128 devices in a mesh: row: 16 (over y_hi, x, core), col: 8 (over y_lo, z).
Axes of the slice: x: 4, y: 4 (y_hi: 2, y_lo: 2; y = y_hi * 2 + y_lo), z: 4, core: 2. Of those that a mesh axis runs over, the one named last changes fastest.
Arguments:
- window_rows: bfloat16 [2048, 65536], P('row', 'col'), may hold values from -6 to 6
- omega_cols: bfloat16 [512, 2048], P(None, 'row'), may hold values from -0.125 to 0.125
- psi_rows: bfloat16 [65536, 1024], P(('col', 'row')), may hold values from -0.09375 to 0.09375
- upsilon_rows: bfloat16 [65536, 2048], P(('col', 'row')), may hold values from -0.09375 to 0.09375
- phi_cols: bfloat16 [2048, 2048], P(None, 'row'), may hold values from -0.125 to 0.125
- range_old: float32 [512, 65536], P(None, ('col', 'row')), may hold values from -6 to 6
- core_old: float32 [2048, 2048], P('row', 'col'), may hold values from -6 to 6
Outputs:
- range_sketch: float32 [512, 65536], P(None, ('col', 'row'))
- corange_sketch: float32 [2048, 1024], P('row', 'col')
- core_sketch: float32 [2048, 2048], P('row', 'col')
The draws below stay inside these ranges and needn't reach their ends.
All inputs are finite; a program needn't handle non-finite values.
Results may differ from the reference program's by a relative error of at most 0.0022.
Values may be sent and summed in bfloat16 or wider, within the bound.
No kernel may reach another device: no remote copies, remote signals or barrier semaphores. Data moves between devices by JAX's collectives and lax.ppermute only.
A program may use at most 128 MiB of HBM per device.

```python
import jax
import jax.numpy as jnp

NCOLS = 65536
K = 512
L = 1024
S = 2048
WINDOW = 2048


def with_spikes(result, own_key, source, target, blocks, factor):
    def block_of(axis_at):
        return (jnp.arange(result.shape[axis_at]) // (result.shape[axis_at] // blocks)).reshape((-1,) + (1,) * (result.ndim - 1 - axis_at))

    first = jax.random.permutation(own_key, blocks)[block_of(target)]
    far = (block_of(target) + blocks // 2) % blocks
    return jnp.where((block_of(source) == first) | (block_of(source) == far), factor * result, result)


def block_levels(rng, shape, split, least, largest):
    factor_of = 1.0
    for position, parts in split:
        heights = jax.random.uniform(jax.random.fold_in(jax.random.fold_in(rng, 6), position), (parts,), jnp.float32, least / len(split), largest / len(split))
        factor_of = factor_of * jnp.repeat(jnp.exp(heights), shape[position] // parts).reshape((-1,) + (1,) * (len(shape) - 1 - position))
    return factor_of


def gaussian(own_key, extent, deviation, most, shards=(), kind=jnp.bfloat16):
    result = deviation * jax.random.normal(own_key, extent, jnp.float32)
    if shards:
        result = result * block_levels(own_key, extent, shards, -0.22, 0.18)
    return jnp.clip(result, -most, most).astype(kind)


def bell_draw_with(key, dims, deviation, bound, pieces, heavy, dtype=jnp.bfloat16):
    result = deviation * jax.random.normal(key, dims, jnp.float32)
    if pieces:
        result = result * block_levels(key, dims, pieces, -0.22, 0.18)
    return jnp.clip(with_spikes(result, jax.random.fold_in(key, 3), *heavy), -bound, bound).astype(dtype)


def setup_inputs(seed: int = 0) -> dict:
    key_list = jax.random.split(jax.random.key(seed), 8)
    return {
        "window_rows": gaussian(key_list[0], (WINDOW, NCOLS), 1.0, 6.0, ((0, 16), (1, 8))),
        "omega_cols": gaussian(key_list[1], (K, WINDOW), WINDOW ** -0.5, 0.125, ((1, 16),)),
        "psi_rows": bell_draw_with(key_list[2], (NCOLS, L), NCOLS ** -0.5, 0.09375, ((0, 128),), (0, 1, 128, 5.5)),
        "upsilon_rows": bell_draw_with(key_list[3], (NCOLS, S), NCOLS ** -0.5, 0.09375, ((0, 128),), (0, 1, 128, 5.5)),
        "phi_cols": gaussian(key_list[4], (S, WINDOW), WINDOW ** -0.5, 0.125, ((1, 16),)),
        "range_old": gaussian(key_list[5], (K, NCOLS), 1.0, 6.0, ((1, 128),), jnp.float32),
        "core_old": gaussian(key_list[6], (S, S), 1.0, 6.0, ((0, 16), (1, 8)), jnp.float32),
    }


def reference(window_rows, omega_cols, psi_rows, upsilon_rows, phi_cols, range_old, core_old):
    range_sketch = range_old + jnp.dot(omega_cols, window_rows, preferred_element_type=jnp.float32)
    corange_sketch = jnp.dot(window_rows, psi_rows, preferred_element_type=jnp.float32)
    sketched = jnp.dot(window_rows, upsilon_rows, preferred_element_type=jnp.float32).astype(jnp.bfloat16)
    core_sketch = core_old + jnp.dot(phi_cols, sketched, preferred_element_type=jnp.float32)
    return range_sketch, corange_sketch, core_sketch
```

```python
import jax
import jax.numpy as jnp
from jax import lax
from jax.sharding import Mesh, PartitionSpec as P

PLANE = ("yh", "x")
TILE = ("yh", "x", "yl")
WIRE = jnp.float16
NEAR = 64.0
FAR = 16.0


def shift(value, axis, by):
    n = lax.axis_size(axis)
    return lax.ppermute(value, axis, [(i, (i + by) % n) for i in range(n)])


def swap(value):
    return lax.ppermute(value, "k", [(0, 1), (1, 0)])


def dot(a, b):
    return jnp.dot(a, b, preferred_element_type=jnp.float32)


def shards(window_rows, omega_cols, psi_rows, upsilon_rows, phi_cols, range_old, core_old):
    k = lax.axis_index("k")
    z = lax.axis_index("z")
    rows, cols = window_rows.shape
    own = cols // 16
    psi_other = swap(psi_rows)
    ups_other = swap(upsilon_rows)

    pieces = window_rows.reshape(rows, 8, 2, own)
    pieces = jnp.where(k == 0, pieces, pieces[:, :, ::-1, :])
    pieces = jnp.moveaxis(pieces.reshape(rows, 8, 2 * own), 1, 0)
    relaid = lax.all_to_all(pieces, PLANE, 0, 0, tiled=True).reshape(8 * rows, 2 * own)

    ups = jnp.concatenate([upsilon_rows, ups_other], axis=0)
    ups = ups.reshape(2 * own, 2, 4, -1)
    wide = ups.shape[-1]

    def part(at):
        piece = lax.dynamic_slice_in_dim(ups, (z + at) % 4, 1, 2).reshape(2 * own, 2 * wide)
        return dot(relaid, piece)

    sent = [shift((NEAR * part(at)).astype(WIRE), "z", at) for at in (2, 1, 3)]
    mine = part(0)

    psi = jnp.concatenate([psi_rows, psi_other], axis=0)
    co = (NEAR * dot(relaid, psi)).astype(WIRE)
    co = co.reshape(8, rows, 2, -1).swapaxes(1, 2).reshape(16, rows, -1)
    co = lax.all_to_all(co, TILE, 0, 0, tiled=True)
    co = jnp.sum(co.astype(jnp.float32), axis=0) * (1.0 / NEAR)

    omega = lax.all_to_all(jnp.broadcast_to(omega_cols[None], (8,) + omega_cols.shape), PLANE, 0, 0, tiled=True)
    omega = jnp.moveaxis(omega, 0, 1).reshape(omega_cols.shape[0], -1)
    phi = lax.all_to_all(phi_cols.reshape(8, -1, phi_cols.shape[1]), PLANE, 0, 0, tiled=True)
    phi = jnp.moveaxis(phi, 0, 1).reshape(-1, 8 * phi_cols.shape[1])

    range_mine = dot(omega, relaid[:, :own])
    range_sketch = range_old + range_mine + swap(dot(omega, relaid[:, own:]))

    total = mine + (1.0 / NEAR) * sum(s.astype(jnp.float32) for s in sent)
    sk = (FAR * total).astype(WIRE).reshape(8, rows, 2, wide).swapaxes(1, 2).reshape(16, rows, wide)
    sk = lax.all_to_all(sk, TILE, 0, 0, tiled=True)
    sk = (jnp.sum(sk.astype(jnp.float32), axis=0) * (1.0 / FAR)).astype(jnp.bfloat16)
    sk = lax.all_to_all(jnp.broadcast_to(sk[None], (8,) + sk.shape), PLANE, 0, 0, tiled=True)
    term = dot(phi, sk.reshape(8 * rows, wide))
    here = lax.dynamic_slice_in_dim(term, k * rows, rows, 0)
    there = lax.dynamic_slice_in_dim(term, (1 - k) * rows, rows, 0)
    core_sketch = core_old + here + swap(there)

    co = jnp.moveaxis(co.reshape(rows, 4, -1), 1, 0)
    corange_sketch = jnp.sum(lax.all_to_all(co, "z", 0, 0, tiled=True), axis=0)
    return (range_sketch, corange_sketch, core_sketch)


def solution(mesh):
    fine = Mesh(mesh.devices.reshape(2, 4, 2, 2, 4), ("yh", "x", "k", "yl", "z"))
    row = ("yh", "x", "k")
    col = ("yl", "z")
    placed = (
        P(row, col),
        P(None, row),
        P(col + row, None),
        P(col + row, None),
        P(None, row),
        P(None, col + row),
        P(row, col),
    )
    return jax.shard_map(
        shards,
        mesh=fine,
        in_specs=placed,
        out_specs=(P(None, col + row), P(row, col), P(row, col)),
        check_vma=False,
    )
```

```python
import jax
import jax.numpy as jnp
from jax import lax
from jax.sharding import Mesh, PartitionSpec as P


PLANE = ("yh", "x")
TILE = ("yh", "x", "yl")
WIRE = jnp.float16
NEAR = 64.0
FAR = 16.0


def shift(value, axis, by):
    n = lax.axis_size(axis)
    return lax.ppermute(value, axis, [(i, (i + by) % n) for i in range(n)])


def swap(value):
    return lax.ppermute(value, "k", [(0, 1), (1, 0)])


def dot(a, b):
    return jnp.dot(a, b, preferred_element_type=jnp.float32)


def after(value, *others):
    return lax.optimization_barrier((value,) + others)[0]


def body(window_rows, omega_cols, psi_rows, upsilon_rows, phi_cols, range_old, core_old):
    k = lax.axis_index("k")
    z = lax.axis_index("z")
    rows, cols = window_rows.shape
    own = cols // 16
    psi_other = swap(psi_rows)
    ups_other = swap(upsilon_rows)

    pieces = jnp.stack([window_rows[:, i * 2 * own : (i + 1) * 2 * own] for i in range(8)])
    relaid = lax.all_to_all(pieces, PLANE, 0, 0, tiled=True).reshape(8 * rows, 2 * own)

    def both(mine, theirs):
        return jnp.concatenate([jnp.where(k == 0, mine, theirs), jnp.where(k == 0, theirs, mine)], axis=0)

    wide = upsilon_rows.shape[1] // 8

    def part(at):
        start = (z + at) % 4 * wide
        cut = [
            jnp.concatenate(
                [lax.dynamic_slice_in_dim(u, start + yl * 4 * wide, wide, 1) for yl in range(2)], axis=1
            )
            for u in (upsilon_rows, ups_other)
        ]
        return both(*cut)

    b = [part(at) for at in range(4)]
    psi = both(psi_rows, psi_other)
    held = lax.optimization_barrier((relaid, psi) + tuple(b))
    relaid, psi, b = held[0], held[1], held[2:]
    sent = []
    for at in (2, 1, 3):
        share = (NEAR * dot(relaid, b[at])).astype(WIRE)
        sent.append(shift(share, "z", at))

    co = (NEAR * dot(relaid, psi)).astype(WIRE)
    co = lax.all_to_all(co.reshape(16, rows // 2, -1), TILE, 0, 0, tiled=True)
    mine = lax.optimization_barrier(dot(relaid, b[0]))
    co = jnp.sum(co.astype(jnp.float32), axis=0) * (1.0 / NEAR)

    small = jnp.concatenate(
        [jnp.broadcast_to(omega_cols[None], (8,) + omega_cols.shape), phi_cols.reshape(8, -1, phi_cols.shape[1])], axis=1
    )
    small = lax.all_to_all(after(small, co), PLANE, 0, 0, tiled=True)
    split = omega_cols.shape[0]
    omega = jnp.moveaxis(small[:, :split], 0, 1).reshape(split, -1)
    phi = jnp.moveaxis(small[:, split:], 0, 1).reshape(-1, 8 * phi_cols.shape[1])

    kept = lax.dynamic_slice_in_dim(relaid, k * own, own, 1)
    given = lax.dynamic_slice_in_dim(relaid, (1 - k) * own, own, 1)
    range_sketch = range_old + dot(omega, kept) + swap(dot(omega, given))

    narrow = co.shape[1] // 8
    co = jnp.stack([co[:, i * narrow : (i + 1) * narrow] for i in range(8)])
    co = lax.all_to_all(co, ("yl", "z"), 0, 0, tiled=True)
    co = co.reshape(2, 4, rows // 2, narrow)
    corange_sketch = jnp.concatenate([jnp.sum(co[0], axis=0), jnp.sum(co[1], axis=0)], axis=0)

    held = lax.optimization_barrier((mine, range_sketch, corange_sketch) + tuple(sent))
    mine, range_sketch, corange_sketch = held[:3]
    total = mine + (1.0 / NEAR) * sum(s.astype(jnp.float32) for s in held[3:])
    sk = (FAR * total).astype(WIRE).reshape(16, rows // 2, 2 * wide)
    sk = lax.all_to_all(sk, TILE, 0, 0, tiled=True)
    sk = (jnp.sum(sk.astype(jnp.float32), axis=0) * (1.0 / FAR)).astype(jnp.bfloat16)
    sk = jnp.stack([sk[:, :wide], sk[:, wide:]])
    sk = jnp.broadcast_to(sk[None], (8,) + sk.shape).reshape(16, rows // 2, wide)
    sk = lax.all_to_all(sk, TILE, 0, 0, tiled=True)
    term = dot(phi, sk.reshape(8 * rows, wide))
    here = lax.dynamic_slice_in_dim(term, k * rows, rows, 0)
    there = lax.dynamic_slice_in_dim(term, (1 - k) * rows, rows, 0)
    core_sketch = core_old + here + swap(there)
    return (range_sketch, corange_sketch, core_sketch)


def solution(mesh):
    fine = Mesh(mesh.devices.reshape(2, 4, 2, 2, 4), ("yh", "x", "k", "yl", "z"))
    row = ("yh", "x", "k")
    col = ("yl", "z")
    placed = (
        P(row, col),
        P(None, row),
        P(col + row, None),
        P(col + row, None),
        P(None, row),
        P(None, col + row),
        P(row, col),
    )
    return jax.shard_map(
        body,
        mesh=fine,
        in_specs=placed,
        out_specs=(P(None, col + row), P(row, col), P(row, col)),
        check_vma=False,
    )
```

```python
import jax
import jax.numpy as jnp
from jax import lax
from jax.experimental import pallas as pl
from jax.sharding import Mesh, PartitionSpec as P


PLANE = ("yh", "x")
TILE = ("yh", "x", "yl")
WIRE = jnp.float16
NEAR = 64.0
FAR = 16.0


def shift(value, axis, by):
    n = lax.axis_size(axis)
    return lax.ppermute(value, axis, [(i, (i + by) % n) for i in range(n)])


def swap(value, axis="k"):
    return lax.ppermute(value, axis, [(0, 1), (1, 0)])


def dot(a, b):
    return jnp.dot(a, b, preferred_element_type=jnp.float32)


def tied(*values):
    return lax.optimization_barrier(values)


def cut_columns(value, count):
    rows, cols = value.shape
    wide = cols // count

    def move(src, dst):
        dst[0] = src[...]

    return pl.pallas_call(
        move,
        grid=(count,),
        in_specs=[pl.BlockSpec((rows, wide), lambda i: (0, i))],
        out_specs=pl.BlockSpec((1, rows, wide), lambda i: (i, 0, 0)),
        out_shape=jax.ShapeDtypeStruct((count, rows, wide), value.dtype),
    )(value)


def exchange(value, axes):
    return lax.all_to_all(value, axes, 0, 0, tiled=True)


def body(window_rows, omega_cols, psi_rows, upsilon_rows, phi_cols, range_old, core_old):
    k = lax.axis_index("k")
    z = lax.axis_index("z")
    yl = lax.axis_index("yl")
    rows, cols = window_rows.shape
    own = cols // 16
    ups_other = swap(upsilon_rows)
    psi_other = swap(psi_rows)

    relaid = exchange(cut_columns(window_rows, 8), PLANE).reshape(8 * rows, 2 * own)

    def both(mine, theirs):
        return jnp.concatenate([jnp.where(k == 0, mine, theirs), jnp.where(k == 0, theirs, mine)], axis=0)

    def pick(value, at, wide):
        start = (z + at) % 4 * wide
        return jnp.concatenate(
            [lax.dynamic_slice_in_dim(value, start + half * 4 * wide, wide, 1) for half in range(2)], axis=1
        )

    wide = upsilon_rows.shape[1] // 8
    b = [both(pick(upsilon_rows, at, wide), pick(ups_other, at, wide)) for at in range(4)]
    psi = both(psi_rows, psi_other)
    split = omega_cols.shape[0]
    small = jnp.concatenate(
        [jnp.broadcast_to(omega_cols[None], (8,) + omega_cols.shape), phi_cols.reshape(8, -1, phi_cols.shape[1])], axis=1
    )
    relaid, psi, small, *b = tied(relaid, psi, small, *b)

    small = exchange(small, PLANE)
    sent = []
    for at in (2, 1, 3):
        share = (NEAR * dot(relaid, b[at])).astype(WIRE)
        sent.append(shift(share, "z", at))

    co = (NEAR * dot(relaid, psi)).astype(WIRE)
    co, small = tied(co, small)
    co = exchange(co.reshape(16, rows // 2, -1), TILE)
    mine = dot(relaid, b[0])
    co = jnp.sum(co.astype(jnp.float32), axis=0) * (1.0 / NEAR)

    mine, co, *sent = tied(mine, co, *sent)
    total = mine + (1.0 / NEAR) * sum(s.astype(jnp.float32) for s in sent)
    sk = (FAR * total).astype(WIRE).reshape(16, rows // 2, 2 * wide)
    sk = exchange(sk, TILE)

    omega = jnp.moveaxis(small[:, :split], 0, 1).reshape(split, -1)
    phi = jnp.moveaxis(small[:, split:], 0, 1).reshape(-1, 8 * phi_cols.shape[1])
    kept = lax.dynamic_slice_in_dim(relaid, k * own, own, 1)
    given = lax.dynamic_slice_in_dim(relaid, (1 - k) * own, own, 1)
    range_given = dot(omega, given)
    range_kept = dot(omega, kept)
    range_sketch = range_old + range_kept + swap(range_given)

    narrow = co.shape[1] // 8
    others = [shift(pick(co, at, narrow), "z", at) for at in (2, 1, 3)]
    co = pick(co, 0, narrow) + others[0] + others[1] + others[2]
    co_kept = lax.dynamic_slice_in_dim(co, yl * narrow, narrow, 1)
    co_other = swap(lax.dynamic_slice_in_dim(co, (1 - yl) * narrow, narrow, 1), "yl")
    corange_sketch = jnp.concatenate(
        [jnp.where(yl == 0, co_kept, co_other), jnp.where(yl == 0, co_other, co_kept)], axis=0
    )

    sk = (jnp.sum(sk.astype(jnp.float32), axis=0) * (1.0 / FAR)).astype(jnp.bfloat16)
    sk = jnp.stack([sk[:, :wide], sk[:, wide:]])
    sk = jnp.broadcast_to(sk[None], (8,) + sk.shape).reshape(16, rows // 2, wide)
    sk = exchange(sk, TILE)
    term = dot(phi, sk.reshape(8 * rows, wide))
    here = lax.dynamic_slice_in_dim(term, k * rows, rows, 0)
    there = lax.dynamic_slice_in_dim(term, (1 - k) * rows, rows, 0)
    core_sketch = core_old + here + swap(there)
    return (range_sketch, corange_sketch, core_sketch)


def solution(mesh):
    fine = Mesh(mesh.devices.reshape(2, 4, 2, 2, 4), ("yh", "x", "k", "yl", "z"))
    row = ("yh", "x", "k")
    col = ("yl", "z")
    placed = (
        P(row, col),
        P(None, row),
        P(col + row, None),
        P(col + row, None),
        P(None, row),
        P(None, col + row),
        P(row, col),
    )
    return jax.shard_map(
        body,
        mesh=fine,
        in_specs=placed,
        out_specs=(P(None, col + row), P(row, col), P(row, col)),
        check_vma=False,
    )
```

```python
import jax
import jax.numpy as jnp
from jax import lax
from jax.experimental import pallas as pl
from jax.experimental.pallas import tpu as pltpu
from jax.sharding import Mesh, PartitionSpec as P


PLANE = ("yh", "x")
TILE = ("yh", "x", "yl")
WIRE = jnp.float16
NEAR = 64.0
FAR = 16.0


def shift(value, axis, by):
    n = lax.axis_size(axis)
    return lax.ppermute(value, axis, [(i, (i + by) % n) for i in range(n)])


def swap(value, axis="k"):
    return lax.ppermute(value, axis, [(0, 1), (1, 0)])


def dot(a, b):
    return jnp.dot(a, b, preferred_element_type=jnp.float32)


def tied(*values):
    return lax.optimization_barrier(values)


def arrange(window_rows, upsilon_rows, omega_cols, phi_cols, k, z):
    rows, cols = window_rows.shape
    own = cols // 16
    deep, width = upsilon_rows.shape
    wide = width // 8
    split, thin = omega_cols.shape
    tall = phi_cols.shape[0] // 8

    def move(where, window, upsilon, omega, phi, pieces, first, second, third, fourth, small, sems):
        picks = (first, second, third, fourth)
        k, z = where[0], where[1]
        copies = []

        def copy(src, dst):
            copies.append(pltpu.make_async_copy(src, dst, sems.at[len(copies)]))
            copies[-1].start()

        for i in range(8):
            for half in range(2):
                start = pl.multiple_of(2 * i * own + (k + half) % 2 * own, own)
                copy(window.at[:, pl.ds(start, own)], pieces.at[i, :, pl.ds(half * own, own)])
        for at in range(4):
            for half in range(2):
                start = pl.multiple_of((z + at) % 4 * wide + half * 4 * wide, wide)
                copy(upsilon.at[:, pl.ds(start, wide)], picks[at].at[:, pl.ds(half * wide, wide)])
        for i in range(8):
            copy(omega, small.at[i, pl.ds(0, split), :])
            copy(phi.at[pl.ds(i * tall, tall), :], small.at[i, pl.ds(split, tall), :])
        for one in copies:
            one.wait()

    kind = window_rows.dtype
    anywhere = pl.BlockSpec(memory_space=pl.ANY)
    return pl.pallas_call(
        move,
        in_specs=[pl.BlockSpec(memory_space=pltpu.SMEM)] + [anywhere] * 4,
        out_specs=[anywhere] * 6,
        out_shape=[
            jax.ShapeDtypeStruct((8, rows, 2 * own), kind),
            *[jax.ShapeDtypeStruct((deep, 2 * wide), kind)] * 4,
            jax.ShapeDtypeStruct((8, split + tall, thin), kind),
        ],
        scratch_shapes=[pltpu.SemaphoreType.DMA((40,))],
    )(jnp.stack([k, z]).astype(jnp.int32), window_rows, upsilon_rows, omega_cols, phi_cols)


def exchange(value, axes):
    return lax.all_to_all(value, axes, 0, 0, tiled=True)


def body(window_rows, omega_cols, psi_rows, upsilon_rows, phi_cols, range_old, core_old):
    k = lax.axis_index("k")
    z = lax.axis_index("z")
    yl = lax.axis_index("yl")
    rows, cols = window_rows.shape
    own = cols // 16
    wide = upsilon_rows.shape[1] // 8
    split = omega_cols.shape[0]

    pieces, *picks, small = arrange(window_rows, upsilon_rows, omega_cols, phi_cols, k, z)
    picks_other = [None] * 4
    for at in (2, 1, 3, 0):
        picks_other[at] = swap(picks[at])
    relaid = exchange(pieces, PLANE).reshape(8 * rows, 2 * own)
    relaid, *picks_other = tied(relaid, *picks_other)
    psi_other = swap(psi_rows)

    def share(at):
        return dot(relaid, jnp.concatenate([picks[at], picks_other[at]], axis=0))

    sent = []
    for at in (2, 1, 3):
        part = (NEAR * share(at)).astype(WIRE)
        sent.append(shift(part, "z", at))

    small = tied(small, relaid)[0]
    small = exchange(small, PLANE)
    co = (NEAR * dot(relaid, jnp.concatenate([psi_rows, psi_other], axis=0))).astype(WIRE)
    mine = share(0)
    co, small, mine = tied(co, small, mine)
    co = exchange(co.reshape(8, rows, -1), PLANE)
    co = jnp.sum(co.astype(jnp.float32), axis=0) * (1.0 / NEAR)

    mine, co, *sent = tied(mine, co, *sent)
    total = mine + (1.0 / NEAR) * sum(s.astype(jnp.float32) for s in sent)
    sk = (FAR * total).astype(WIRE).reshape(16, rows // 2, 2 * wide)
    sk = exchange(sk, TILE)

    omega = jnp.moveaxis(small[:, :split], 0, 1).reshape(split, -1)
    phi = jnp.moveaxis(small[:, split:], 0, 1).reshape(-1, 8 * phi_cols.shape[1])
    range_given = dot(omega, relaid[:, own:])
    range_kept = dot(omega, relaid[:, :own])
    range_sketch = range_old + range_kept + swap(range_given)

    def pick(value, at, wide):
        start = (z + at) % 4 * wide
        return jnp.concatenate(
            [lax.dynamic_slice_in_dim(value, start + half * 4 * wide, wide, 1) for half in range(2)], axis=1
        )

    narrow = co.shape[1] // 8
    others = [shift(pick(co, at, narrow), "z", at) for at in (2, 1, 3)]
    co = pick(co, 0, narrow) + others[0] + others[1] + others[2]
    co_kept = lax.dynamic_slice_in_dim(co, yl * narrow, narrow, 1)
    corange_sketch = co_kept + swap(lax.dynamic_slice_in_dim(co, (1 - yl) * narrow, narrow, 1), "yl")

    sk = (jnp.sum(sk.astype(jnp.float32), axis=0) * (1.0 / FAR)).astype(jnp.bfloat16)
    sk = jnp.stack([sk[:, :wide], sk[:, wide:]])
    sk = jnp.broadcast_to(sk[None], (8,) + sk.shape).reshape(16, rows // 2, wide)
    sk = exchange(sk, TILE)
    term = dot(phi, sk.reshape(8 * rows, wide))
    here = lax.dynamic_slice_in_dim(term, k * rows, rows, 0)
    there = lax.dynamic_slice_in_dim(term, (1 - k) * rows, rows, 0)
    core_sketch = core_old + here + swap(there)
    return (range_sketch, corange_sketch, core_sketch)


def solution(mesh):
    fine = Mesh(mesh.devices.reshape(2, 4, 2, 2, 4), ("yh", "x", "k", "yl", "z"))
    row = ("yh", "x", "k")
    col = ("yl", "z")
    placed = (
        P(row, col),
        P(None, row),
        P(col + row, None),
        P(col + row, None),
        P(None, row),
        P(None, col + row),
        P(row, col),
    )
    return jax.shard_map(
        body,
        mesh=fine,
        in_specs=placed,
        out_specs=(P(None, col + row), P(row, col), P(row, col)),
        check_vma=False,
    )
```

```python
import jax
import jax.numpy as jnp
from jax import lax
from jax.experimental import pallas as pl
from jax.experimental.pallas import tpu as pltpu
from jax.sharding import Mesh, PartitionSpec as P


PLANE = ("yh", "x")
TILE = ("yh", "x", "yl")
WIRE = jnp.float16
NEAR = 64.0
FAR = 16.0


def shift(value, axis, by):
    n = lax.axis_size(axis)
    return lax.ppermute(value, axis, [(i, (i + by) % n) for i in range(n)])


def swap(value, axis="k"):
    return lax.ppermute(value, axis, [(0, 1), (1, 0)])


def dot(a, b):
    return jnp.dot(a, b, preferred_element_type=jnp.float32)


def tied(*values):
    return lax.optimization_barrier(values)


def arrange(window_rows, upsilon_rows, omega_cols, phi_cols, k, z):
    rows, cols = window_rows.shape
    own = cols // 16
    deep, width = upsilon_rows.shape
    wide = width // 8
    split, thin = omega_cols.shape
    tall = phi_cols.shape[0] // 8

    def move(where, window, upsilon, omega, phi, pieces, first, second, third, fourth, small, w_buf, u_buf, s_buf, sems):
        k, z = where[0], where[1]
        picks = (first, second, third, fourth)
        count = 0

        def copy(src, dst):
            nonlocal count
            made = pltpu.make_async_copy(src, dst, sems.at[count])
            count += 1
            made.start()
            return made

        loads = []
        for i in range(8):
            for half in range(2):
                start = pl.multiple_of(2 * i * own + (k + half) % 2 * own, own)
                loads.append(copy(window.at[:, pl.ds(start, own)], w_buf.at[i, :, pl.ds(half * own, own)]))
        for at in range(4):
            for half in range(2):
                start = pl.multiple_of((z + at) % 4 * wide + half * 4 * wide, wide)
                loads.append(copy(upsilon.at[:, pl.ds(start, wide)], u_buf.at[at, :, pl.ds(half * wide, wide)]))
        turned = omega[...].T
        stores = []
        for i in range(8):
            s_buf[i, :, :split] = turned
            s_buf[i, :, split:] = phi[i * tall : (i + 1) * tall, :].T
            stores.append(copy(s_buf.at[i], small.at[i]))
        for i in range(8):
            loads[2 * i].wait()
            loads[2 * i + 1].wait()
            stores.append(copy(w_buf.at[i], pieces.at[i]))
        for at in range(4):
            loads[16 + 2 * at].wait()
            loads[17 + 2 * at].wait()
            stores.append(copy(u_buf.at[at], picks[at]))
        for one in stores:
            one.wait()

    kind = window_rows.dtype
    anywhere = pl.BlockSpec(memory_space=pl.ANY)
    near = pl.BlockSpec(memory_space=pltpu.VMEM)
    return pl.pallas_call(
        move,
        in_specs=[pl.BlockSpec(memory_space=pltpu.SMEM), anywhere, anywhere, near, near],
        out_specs=[anywhere] * 6,
        out_shape=[
            jax.ShapeDtypeStruct((8, rows, 2 * own), kind),
            *[jax.ShapeDtypeStruct((deep, 2 * wide), kind)] * 4,
            jax.ShapeDtypeStruct((8, thin, split + tall), kind),
        ],
        scratch_shapes=[
            pltpu.VMEM((8, rows, 2 * own), kind),
            pltpu.VMEM((4, deep, 2 * wide), kind),
            pltpu.VMEM((8, thin, split + tall), kind),
            pltpu.SemaphoreType.DMA((44,)),
        ],
    )(jnp.stack([k, z]).astype(jnp.int32), window_rows, upsilon_rows, omega_cols, phi_cols)


def dot_down(a, b):
    return lax.dot_general(a, b, (((0,), (0,)), ((), ())), preferred_element_type=jnp.float32)


def exchange(value, axes):
    return lax.all_to_all(value, axes, 0, 0, tiled=True)


def body(window_rows, omega_cols, psi_rows, upsilon_rows, phi_cols, range_old, core_old):
    k = lax.axis_index("k")
    z = lax.axis_index("z")
    yl = lax.axis_index("yl")
    rows, cols = window_rows.shape
    own = cols // 16
    wide = upsilon_rows.shape[1] // 8
    split = omega_cols.shape[0]

    pieces, *picks, small = arrange(window_rows, upsilon_rows, omega_cols, phi_cols, k, z)
    picks_other = [None] * 4
    for at in (2, 1, 3, 0):
        picks_other[at] = swap(picks[at])
    psi_other = swap(psi_rows)
    relaid = exchange(pieces, PLANE).reshape(8 * rows, 2 * own)
    relaid, psi_other, *picks_other = tied(relaid, psi_other, *picks_other)

    def share(at):
        return dot(relaid, jnp.concatenate([picks[at], picks_other[at]], axis=0))

    sent = []
    for at in (2, 1, 3):
        part = (NEAR * share(at)).astype(WIRE)
        sent.append(shift(part, "z", at))

    small = tied(small, relaid)[0]
    small = exchange(small, PLANE)
    co = (NEAR * dot(relaid, jnp.concatenate([psi_rows, psi_other], axis=0))).astype(WIRE)
    mine = share(0)
    co, small, mine = tied(co, small, mine)
    co = exchange(co.reshape(8, rows, -1), PLANE)
    co = jnp.sum(co.astype(jnp.float32), axis=0) * (1.0 / NEAR)

    mine, co, small, *sent = tied(mine, co, small, *sent)
    total = mine + (1.0 / NEAR) * sum(s.astype(jnp.float32) for s in sent)
    sk = (FAR * total).astype(WIRE).reshape(16, rows // 2, 2 * wide)
    sk = exchange(sk, TILE)

    small = small.reshape(8 * rows, -1)
    omega, phi = small[:, :split], small[:, split:]
    range_given = dot_down(omega, relaid[:, own:])
    range_kept = dot_down(omega, relaid[:, :own])
    range_sketch = range_old + range_kept + swap(range_given)

    def pick(value, at, wide):
        start = (z + at) % 4 * wide
        return jnp.concatenate(
            [lax.dynamic_slice_in_dim(value, start + half * 4 * wide, wide, 1) for half in range(2)], axis=1
        )

    narrow = co.shape[1] // 8
    others = [shift(pick(co, at, narrow), "z", at) for at in (2, 1, 3)]
    co = pick(co, 0, narrow) + others[0] + others[1] + others[2]
    co_kept = lax.dynamic_slice_in_dim(co, yl * narrow, narrow, 1)
    corange_sketch = co_kept + swap(lax.dynamic_slice_in_dim(co, (1 - yl) * narrow, narrow, 1), "yl")

    sk = (jnp.sum(sk.astype(jnp.float32), axis=0) * (1.0 / FAR)).astype(jnp.bfloat16)
    sk = jnp.stack([sk[:, :wide], sk[:, wide:]])
    sk = jnp.broadcast_to(sk[None], (8,) + sk.shape).reshape(16, rows // 2, wide)
    sk = exchange(sk, TILE)
    term = dot_down(phi, sk.reshape(8 * rows, wide))
    here = lax.dynamic_slice_in_dim(term, k * rows, rows, 0)
    there = lax.dynamic_slice_in_dim(term, (1 - k) * rows, rows, 0)
    core_sketch = core_old + here + swap(there)
    return (range_sketch, corange_sketch, core_sketch)


def solution(mesh):
    fine = Mesh(mesh.devices.reshape(2, 4, 2, 2, 4), ("yh", "x", "k", "yl", "z"))
    row = ("yh", "x", "k")
    col = ("yl", "z")
    placed = (
        P(row, col),
        P(None, row),
        P(col + row, None),
        P(col + row, None),
        P(None, row),
        P(None, col + row),
        P(row, col),
    )
    return jax.shard_map(
        body,
        mesh=fine,
        in_specs=placed,
        out_specs=(P(None, col + row), P(row, col), P(row, col)),
        check_vma=False,
    )
```

```python
import jax
import jax.numpy as jnp
from jax import lax
from jax.experimental import pallas as pl
from jax.experimental.pallas import tpu as pltpu
from jax.sharding import Mesh, PartitionSpec as P


PLANE = ("yh", "x")
TILE = ("yh", "x", "yl")
WIRE = jnp.float16
NEAR = 64.0
FAR = 16.0


def shift(value, axis, by):
    n = lax.axis_size(axis)
    return lax.ppermute(value, axis, [(i, (i + by) % n) for i in range(n)])


def swap(value, axis="k"):
    return lax.ppermute(value, axis, [(0, 1), (1, 0)])


def dot(a, b):
    return jnp.dot(a, b, preferred_element_type=jnp.float32)


def tied(*values):
    return lax.optimization_barrier(values)


def launcher(sems):
    started = []

    def copy(src, dst):
        made = pltpu.make_async_copy(src, dst, sems.at[len(started)])
        started.append(made)
        made.start()
        return made

    return copy


ANYWHERE = pl.BlockSpec(memory_space=pl.ANY)
NEARBY = pl.BlockSpec(memory_space=pltpu.VMEM)
SCALARS = pl.BlockSpec(memory_space=pltpu.SMEM)


def cut_window(where, window_rows):
    rows, cols = window_rows.shape
    own = cols // 16

    def move(where, window, pieces, buf, sems):
        k = where[0]
        copy = launcher(sems)
        loads = []
        for i in range(8):
            for half in range(2):
                start = pl.multiple_of(2 * i * own + (k + half) % 2 * own, own)
                loads.append(copy(window.at[:, pl.ds(start, own)], buf.at[i, :, pl.ds(half * own, own)]))
        stores = []
        for i in range(8):
            loads[2 * i].wait()
            loads[2 * i + 1].wait()
            stores.append(copy(buf.at[i], pieces.at[i]))
        for one in stores:
            one.wait()

    shape = (8, rows, 2 * own)
    return pl.pallas_call(
        move,
        in_specs=[SCALARS, ANYWHERE],
        out_specs=ANYWHERE,
        out_shape=jax.ShapeDtypeStruct(shape, window_rows.dtype),
        scratch_shapes=[pltpu.VMEM(shape, window_rows.dtype), pltpu.SemaphoreType.DMA((24,))],
    )(where, window_rows)


def arrange(where, upsilon_rows, omega_cols, phi_cols):
    deep, width = upsilon_rows.shape
    wide = width // 8
    split, thin = omega_cols.shape
    tall = phi_cols.shape[0] // 8

    def move(where, upsilon, omega, phi, first, second, third, fourth, small, u_buf, s_buf, sems):
        z = where[1]
        picks = (first, second, third, fourth)
        copy = launcher(sems)
        loads = []
        for at in (2, 1, 3, 0):
            for half in range(2):
                start = pl.multiple_of((z + at) % 4 * wide + half * 4 * wide, wide)
                loads.append(copy(upsilon.at[:, pl.ds(start, wide)], u_buf.at[at, :, pl.ds(half * wide, wide)]))
        turned = omega[...].T
        stores = []
        for i in range(8):
            s_buf[i, :, :split] = turned
            s_buf[i, :, split:] = phi[i * tall : (i + 1) * tall, :].T
            stores.append(copy(s_buf.at[i], small.at[i]))
        for place, at in enumerate((2, 1, 3, 0)):
            loads[2 * place].wait()
            loads[2 * place + 1].wait()
            stores.append(copy(u_buf.at[at], picks[at]))
        for one in stores:
            one.wait()

    kind = upsilon_rows.dtype
    return pl.pallas_call(
        move,
        in_specs=[SCALARS, ANYWHERE, NEARBY, NEARBY],
        out_specs=[ANYWHERE] * 5,
        out_shape=[
            *[jax.ShapeDtypeStruct((deep, 2 * wide), kind)] * 4,
            jax.ShapeDtypeStruct((8, thin, split + tall), kind),
        ],
        scratch_shapes=[
            pltpu.VMEM((4, deep, 2 * wide), kind),
            pltpu.VMEM((8, thin, split + tall), kind),
            pltpu.SemaphoreType.DMA((20,)),
        ],
    )(where, upsilon_rows, omega_cols, phi_cols)


def dot_down(a, b):
    return lax.dot_general(a, b, (((0,), (0,)), ((), ())), preferred_element_type=jnp.float32)


def exchange(value, axes):
    return lax.all_to_all(value, axes, 0, 0, tiled=True)


def body(window_rows, omega_cols, psi_rows, upsilon_rows, phi_cols, range_old, core_old):
    k = lax.axis_index("k")
    z = lax.axis_index("z")
    yl = lax.axis_index("yl")
    rows, cols = window_rows.shape
    own = cols // 16
    wide = upsilon_rows.shape[1] // 8
    split = omega_cols.shape[0]

    where = jnp.stack([k, z]).astype(jnp.int32)
    pieces = cut_window(where, window_rows)
    relaid = exchange(pieces, PLANE).reshape(8 * rows, 2 * own)
    *picks, small = arrange(where, upsilon_rows, omega_cols, phi_cols)
    psi_other = swap(psi_rows)
    picks_other = [None] * 4
    for at in (2, 1, 3, 0):
        picks_other[at] = swap(picks[at])
    relaid, psi_other, *picks_other = tied(relaid, psi_other, *picks_other)

    def share(at):
        return dot(relaid, jnp.concatenate([picks[at], picks_other[at]], axis=0))

    co = (NEAR * dot(relaid, jnp.concatenate([psi_rows, psi_other], axis=0))).astype(WIRE)
    co = exchange(co.reshape(8, rows, -1), PLANE)

    sent = []
    for at in (2, 1, 3):
        part = (NEAR * share(at)).astype(WIRE)
        sent.append(shift(part, "z", at))
    mine = share(0)

    co, small = tied(co, small)
    small = exchange(small, PLANE)
    co = jnp.sum(co.astype(jnp.float32), axis=0) * (1.0 / NEAR)

    def pick(value, at, wide):
        start = (z + at) % 4 * wide
        return jnp.concatenate(
            [lax.dynamic_slice_in_dim(value, start + half * 4 * wide, wide, 1) for half in range(2)], axis=1
        )

    narrow = co.shape[1] // 8
    others = [shift(pick(co, at, narrow), "z", at) for at in (2, 1, 3)]

    mine, small, *sent = tied(mine, small, *sent)
    total = mine + (1.0 / NEAR) * sum(s.astype(jnp.float32) for s in sent)
    sk = (FAR * total).astype(WIRE).reshape(16, rows // 2, 2 * wide)
    sk = exchange(sk, TILE)

    small = small.reshape(8 * rows, -1)
    omega, phi = small[:, :split], small[:, split:]
    range_given = dot_down(omega, relaid[:, own:])
    range_kept = dot_down(omega, relaid[:, :own])
    range_sketch = range_old + range_kept + swap(range_given)

    co = pick(co, 0, narrow) + others[0] + others[1] + others[2]
    co_kept = lax.dynamic_slice_in_dim(co, yl * narrow, narrow, 1)
    corange_sketch = co_kept + swap(lax.dynamic_slice_in_dim(co, (1 - yl) * narrow, narrow, 1), "yl")

    sk = (jnp.sum(sk.astype(jnp.float32), axis=0) * (1.0 / FAR)).astype(jnp.bfloat16)
    sk = jnp.stack([sk[:, :wide], sk[:, wide:]])
    sk = jnp.broadcast_to(sk[None], (8,) + sk.shape).reshape(16, rows // 2, wide)
    sk = exchange(sk, TILE)
    term = dot_down(phi, sk.reshape(8 * rows, wide))
    here = lax.dynamic_slice_in_dim(term, k * rows, rows, 0)
    there = lax.dynamic_slice_in_dim(term, (1 - k) * rows, rows, 0)
    core_sketch = core_old + here + swap(there)
    return (range_sketch, corange_sketch, core_sketch)


def solution(mesh):
    fine = Mesh(mesh.devices.reshape(2, 4, 2, 2, 4), ("yh", "x", "k", "yl", "z"))
    row = ("yh", "x", "k")
    col = ("yl", "z")
    placed = (
        P(row, col),
        P(None, row),
        P(col + row, None),
        P(col + row, None),
        P(None, row),
        P(None, col + row),
        P(row, col),
    )
    return jax.shard_map(
        body,
        mesh=fine,
        in_specs=placed,
        out_specs=(P(None, col + row), P(row, col), P(row, col)),
        check_vma=False,
    )
```

```python
import jax
import jax.numpy as jnp
from jax import lax
from jax.experimental import pallas as pl
from jax.experimental.pallas import tpu as pltpu
from jax.sharding import Mesh, PartitionSpec as P


PLANE = ("yh", "x")
TILE = ("yh", "x", "yl")
WIRE = jnp.float16
NEAR = 64.0
FAR = 16.0


def shift(value, axis, by):
    n = lax.psum(1, axis)
    return lax.ppermute(value, axis, [(i, (i + by) % n) for i in range(n)])


def swap(value, axis="k"):
    return lax.ppermute(value, axis, [(0, 1), (1, 0)])


def dot(a, b):
    return jnp.dot(a, b, preferred_element_type=jnp.float32)


def tied(*values):
    return lax.optimization_barrier(values)


def launcher(sems):
    started = []

    def copy(src, dst):
        made = pltpu.make_async_copy(src, dst, sems.at[len(started)])
        started.append(made)
        made.start()
        return made

    return copy


ANYWHERE = pl.BlockSpec(memory_space=pl.ANY)
NEARBY = pl.BlockSpec(memory_space=pltpu.VMEM)
SCALARS = pl.BlockSpec(memory_space=pltpu.SMEM)


def cut_window(where, window_rows):
    rows, cols = window_rows.shape
    own = cols // 16

    def move(where, window, pieces, buf, sems):
        k = where[0]
        copy = launcher(sems)
        loads = []
        for i in range(8):
            for half in range(2):
                start = pl.multiple_of(2 * i * own + (k + half) % 2 * own, own)
                loads.append(copy(window.at[:, pl.ds(start, own)], buf.at[i, :, pl.ds(half * own, own)]))
        stores = []
        for i in range(8):
            loads[2 * i].wait()
            loads[2 * i + 1].wait()
            stores.append(copy(buf.at[i], pieces.at[i]))
        for one in stores:
            one.wait()

    shape = (8, rows, 2 * own)
    return pl.pallas_call(
        move,
        in_specs=[SCALARS, ANYWHERE],
        out_specs=ANYWHERE,
        out_shape=jax.ShapeDtypeStruct(shape, window_rows.dtype),
        scratch_shapes=[pltpu.VMEM(shape, window_rows.dtype), pltpu.SemaphoreType.DMA((24,))],
    )(where, window_rows)


def arrange(where, upsilon_rows, omega_cols, phi_cols):
    deep, width = upsilon_rows.shape
    wide = width // 8
    split, thin = omega_cols.shape
    tall = phi_cols.shape[0] // 8

    def move(where, upsilon, omega, phi, first, second, third, fourth, *rest):
        *small, u_buf, s_buf, sems = rest
        z, place_here = where[1], where[2]
        picks = (first, second, third, fourth)
        copy = launcher(sems)
        loads = []
        for at in (2, 1, 3, 0):
            for half in range(2):
                start = pl.multiple_of((z + at) % 4 * wide + half * 4 * wide, wide)
                loads.append(copy(upsilon.at[:, pl.ds(start, wide)], u_buf.at[at, :, pl.ds(half * wide, wide)]))
        turned = omega[...].T
        stores = []
        for i in range(8):
            start = pl.multiple_of((place_here + i) % 8 * tall, tall)
            s_buf[i, :, :split] = turned
            s_buf[i, :, split:] = phi[pl.ds(start, tall), :].T
            stores.append(copy(s_buf.at[i], small[i]))
        for place, at in enumerate((2, 1, 3, 0)):
            loads[2 * place].wait()
            loads[2 * place + 1].wait()
            stores.append(copy(u_buf.at[at], picks[at]))
        for one in stores:
            one.wait()

    kind = upsilon_rows.dtype
    return pl.pallas_call(
        move,
        in_specs=[SCALARS, ANYWHERE, NEARBY, NEARBY],
        out_specs=[ANYWHERE] * 12,
        out_shape=[
            *[jax.ShapeDtypeStruct((deep, 2 * wide), kind)] * 4,
            *[jax.ShapeDtypeStruct((thin, split + tall), kind)] * 8,
        ],
        scratch_shapes=[
            pltpu.VMEM((4, deep, 2 * wide), kind),
            pltpu.VMEM((8, thin, split + tall), kind),
            pltpu.SemaphoreType.DMA((20,)),
        ],
    )(where, upsilon_rows, omega_cols, phi_cols)


def assemble(where, blocks):
    shape = (8,) + blocks[0].shape

    def move(where, *refs):
        *parts, whole, buf, sems = refs
        copy = launcher(sems)
        loads = [copy(parts[i], buf.at[(where[2] + 8 - i) % 8]) for i in range(8)]
        for one in loads:
            one.wait()
        copy(buf, whole).wait()

    return pl.pallas_call(
        move,
        in_specs=[SCALARS] + [ANYWHERE] * 8,
        out_specs=ANYWHERE,
        out_shape=jax.ShapeDtypeStruct(shape, blocks[0].dtype),
        scratch_shapes=[pltpu.VMEM(shape, blocks[0].dtype), pltpu.SemaphoreType.DMA((9,))],
    )(where, *blocks)


def dot_down(a, b):
    return lax.dot_general(a, b, (((0,), (0,)), ((), ())), preferred_element_type=jnp.float32)


def exchange(value, axes):
    return lax.all_to_all(value, axes, 0, 0, tiled=True)


def body(window_rows, omega_cols, psi_rows, upsilon_rows, phi_cols, range_old, core_old):
    k = lax.axis_index("k")
    z = lax.axis_index("z")
    yl = lax.axis_index("yl")
    rows, cols = window_rows.shape
    own = cols // 16
    wide = upsilon_rows.shape[1] // 8
    split = omega_cols.shape[0]

    where = jnp.stack([k, z, lax.axis_index(PLANE)]).astype(jnp.int32)
    pieces = cut_window(where, window_rows)
    relaid = exchange(pieces, PLANE).reshape(8 * rows, 2 * own)
    arranged = arrange(where, upsilon_rows, omega_cols, phi_cols)
    picks, small = arranged[:4], arranged[4:]
    psi_other = swap(psi_rows)
    picks_other = [None] * 4
    for at in (2, 1, 3, 0):
        picks_other[at] = swap(picks[at])
    relaid, psi_other, *picks_other = tied(relaid, psi_other, *picks_other)

    def share(at):
        return dot(relaid, jnp.concatenate([picks[at], picks_other[at]], axis=0))

    sent = []
    for at in (2, 1, 3):
        part = (NEAR * share(at)).astype(WIRE)
        sent.append(shift(part, "z", at))
    co = (NEAR * dot(relaid, jnp.concatenate([psi_rows, psi_other], axis=0))).astype(WIRE)
    co = exchange(co.reshape(8, rows, -1), PLANE)
    mine = share(0)
    small = [small[0]] + [shift(small[by], PLANE, by) for by in range(1, 8)]
    co = jnp.sum(co.astype(jnp.float32), axis=0) * (1.0 / NEAR)

    def pick(value, at, wide):
        start = (z + at) % 4 * wide
        return jnp.concatenate(
            [lax.dynamic_slice_in_dim(value, start + half * 4 * wide, wide, 1) for half in range(2)], axis=1
        )

    narrow = co.shape[1] // 8
    others = [shift(pick(co, at, narrow), "z", at) for at in (2, 1, 3)]

    mine, co, *sent = tied(mine, co, *sent)
    total = mine + (1.0 / NEAR) * sum(s.astype(jnp.float32) for s in sent)
    sk = (FAR * total).astype(WIRE).reshape(16, rows // 2, 2 * wide)
    sk = exchange(sk, TILE)

    small = assemble(where, small).reshape(8 * rows, -1)
    omega, phi = small[:, :split], small[:, split:]
    range_given = dot_down(omega, relaid[:, own:])
    range_kept = dot_down(omega, relaid[:, :own])
    range_sketch = range_old + range_kept + swap(range_given)

    co = pick(co, 0, narrow) + others[0] + others[1] + others[2]
    co_kept = lax.dynamic_slice_in_dim(co, yl * narrow, narrow, 1)
    corange_sketch = co_kept + swap(lax.dynamic_slice_in_dim(co, (1 - yl) * narrow, narrow, 1), "yl")

    sk = (jnp.sum(sk.astype(jnp.float32), axis=0) * (1.0 / FAR)).astype(jnp.bfloat16)
    sk = jnp.stack([sk[:, :wide], sk[:, wide:]])
    sk = jnp.broadcast_to(sk[None], (8,) + sk.shape).reshape(16, rows // 2, wide)
    sk = exchange(sk, TILE)
    term = dot_down(phi, sk.reshape(8 * rows, wide))
    here = lax.dynamic_slice_in_dim(term, k * rows, rows, 0)
    there = lax.dynamic_slice_in_dim(term, (1 - k) * rows, rows, 0)
    core_sketch = core_old + here + swap(there)
    return (range_sketch, corange_sketch, core_sketch)


def solution(mesh):
    fine = Mesh(mesh.devices.reshape(2, 4, 2, 2, 4), ("yh", "x", "k", "yl", "z"))
    row = ("yh", "x", "k")
    col = ("yl", "z")
    placed = (
        P(row, col),
        P(None, row),
        P(col + row, None),
        P(col + row, None),
        P(None, row),
        P(None, col + row),
        P(row, col),
    )
    return jax.shard_map(
        body,
        mesh=fine,
        in_specs=placed,
        out_specs=(P(None, col + row), P(row, col), P(row, col)),
        check_vma=False,
    )
```
